512 devices in a mesh: tx: 8 (over y, core), ty: 16 (over z), pb: 4 (over x).
Axes of the slice: x: 4, y: 4, z: 16, core: 2. Of those that a mesh axis runs over, the one named last changes fastest.
Arguments:
- features: bfloat16 [32, 32, 64, 512], P(None, 'tx', 'ty', 'pb'), may hold values from -6 to 6
- conv_weight: bfloat16 [27, 32, 32], replicated, may hold values from -0.21875 to 0.21875
- mask_weight: bfloat16 [32, 128], replicated, may hold values from -1 to 1
- block_mask: int32 [8, 16, 64], P('tx', 'ty', 'pb'), may hold values 0 or 1
- voxel_mask: int32 [32, 64, 512], P('tx', 'ty', 'pb'), may hold values 0 or 1
- voxel_labels: int32 [32, 64, 512], P('tx', 'ty', 'pb'), may hold values from 0 to 3
- queries: bfloat16 [16384, 128], P(('tx', 'ty', 'pb')), may hold values from -1.5 to 1.5
- routes: int32 [16384, 4], replicated, may hold values from 0 to 127, all different within a row; in each aligned block of 32 rows (0 to 31, 32 to 63, ...) at most 2 rows name the same one
- matched: int32 [16384], replicated, may hold values from 0 to 3
Outputs:
- query_grads: float32 [16384, 128], P(('tx', 'ty', 'pb'))
The draws below stay inside these ranges and needn't reach their ends.
Inputs may be any that keep to these rules, and one draw needn't show every extreme that they name: `routes`: each row names 4 different tiles. Among the 32 rows of one device no tile is named by more than 2 rows, and in every draw some tile is named by exactly 2 rows of some device.
All inputs are finite; a program needn't handle non-finite values. No bound on the sum of `block_mask` or of `voxel_mask` on one device may be relied on, other than what follows from the above.
Results may differ from the reference program's by a relative error of at most 0.00045.
Values may be sent and summed in bfloat16 or wider, within the bound.
No kernel may reach another device: no remote copies, remote signals or barrier semaphores. Data moves between devices by JAX's collectives and lax.ppermute only.
A program may use at most 64 MiB of HBM per device.

```python
import math
import jax
import jax.numpy as jnp
import numpy as np
from jax import lax

CH = 32
MD = 128
BX = 4
BY = 4
BZ = 8
TOP = 4
NINST = 4
CX = 4
CY = 4
Q_DEV = 32
MOST = 2
NQ = 16384
NX = 32
NY = 64
NZ = 512
N_TX = 8
N_TY = 16


def with_ends(values, own_key, low, largest):
    extent = values.shape
    place = [jax.random.randint(jax.random.fold_in(own_key, axis), (), 0, extent[axis]) for axis in range(len(extent))]
    values = values.at[tuple(place)].set(low)
    longest = extent.index(max(extent))
    place[longest] = (place[longest] + 1) % extent[longest]
    return values.at[tuple(place)].set(largest)


def steps_of(rng, extent, pieces, least, top_value):
    loudness, own = 1.0, jax.random.fold_in(rng, 6)
    for axis_at, blocks in pieces:
        steps = jnp.exp(jax.random.uniform(jax.random.fold_in(own, axis_at), (blocks,), jnp.float32, least / len(pieces), top_value / len(pieces)))
        loudness = loudness * jnp.repeat(steps, extent[axis_at] // blocks).reshape([-1 if axis == axis_at else 1 for axis in range(len(extent))])
    return loudness


def routed_block(rng, own, number, rows, amount, top, reach, slope):
    sequence = jax.random.permutation(rng, amount)
    crowded, common = shares(amount, rows * top, reach, slope, True), shares(amount, rows * top, reach, slope, False)
    places = jnp.arange(amount)

    def named(lengths, turn):
        used = int((lengths > 0).sum())
        fixed = max(1, used // 4)
        moved = fixed + (places - fixed + turn * (used - fixed)) % max(1, amount - fixed)
        return jnp.zeros((amount,), jnp.int32).at[sequence[jnp.where(places < fixed, places, moved)]].set(jnp.asarray(lengths, jnp.int32))

    lengths = jnp.where(number % 4 == 0, named(crowded, number // 4), named(common, number - number // 4 - 1))
    mixed = jax.random.permutation(jax.random.fold_in(own, 3), amount)
    giver, receiver = mixed[0:amount // 2 * 2:2], mixed[1:amount // 2 * 2:2]
    slack = jnp.minimum(lengths[giver] - 1, reach - lengths[receiver]) // 2
    slack = jnp.where((giver == sequence[0]) | (receiver == sequence[0]) | (lengths[receiver] == 0), 0, jnp.maximum(slack, 0))
    moved = jax.random.randint(jax.random.fold_in(own, 4), (amount // 2,), 0, 1 << 20) % (slack + 1)
    lengths = lengths.at[giver].add(-moved).at[receiver].add(moved)
    labels = jnp.searchsorted(jnp.cumsum(lengths), jnp.arange(rows * top), side="right").astype(jnp.int32)
    grid = labels.reshape(top, rows).T
    grid = grid[jax.random.permutation(jax.random.fold_in(own, 1), rows)]
    turn = jax.random.randint(jax.random.fold_in(own, 2), (rows, 1), 0, top)
    return jnp.take_along_axis(grid, (jnp.arange(top)[None, :] + turn) % top, axis=1)


def shares(amount, total, most, skew, full):
    loads = [(1 << 20) // math.isqrt(grade ** skew) + 1 for grade in range(1, amount + 1)]
    largest = most if full else min(most, max(-(-total // amount), total * loads[0] // sum(loads)))
    least = 1 if total - largest >= amount - 1 else 0
    counts, surplus = [largest] + [least] * (amount - 1), total - largest - least * (amount - 1)
    while surplus > 0:
        free = [i for i in range(1, amount) if counts[i] < largest] or [i for i in range(1, amount) if counts[i] < most]
        mass, budget = sum([loads[i] for i in free]), surplus
        for i in free:
            more = min(most - counts[i], max(1, budget * loads[i] // mass), surplus)
            counts[i] = counts[i] + more
            surplus = surplus - more
    return np.array(counts)


def centred(stream_key, extent, scale, reach, shards=(), kind=jnp.bfloat16):
    drawn = jax.random.normal(stream_key, extent, jnp.float32) * scale
    if len(shards) > 0:
        drawn = steps_of(stream_key, extent, shards, -0.22, 0.18) * drawn
    return jnp.clip(drawn, min=-reach, max=reach).astype(kind)


def setup_inputs(seed: int = 0) -> dict:
    key_list = jax.random.split(jax.random.key(seed), 10)
    features = centred(key_list[0], (CH, NX, NY, NZ), 1.0, 6.0, ((1, 8), (2, 16), (3, 4)))
    conv_weight = centred(key_list[1], (27, CH, CH), (27 * CH) ** -0.5, 0.21875)
    mask_weight = centred(key_list[2], (CH, MD), CH ** -0.5, 1.0)
    block_mask = with_ends((jax.random.randint(key_list[3], (NX // BX, NY // BY, NZ // BZ), 0, 4) < 3).astype(jnp.int32), jax.random.fold_in(key_list[3], 1), 0, 1)
    voxel_mask = with_ends((jax.random.randint(key_list[4], (NX, NY, NZ), 0, 4) < 3).astype(jnp.int32), jax.random.fold_in(key_list[4], 1), 0, 1)
    voxel_labels = with_ends(jax.random.randint(key_list[5], (NX, NY, NZ), 0, NINST), jax.random.fold_in(key_list[5], 1), 0, NINST - 1).astype(jnp.int32)
    queries = centred(key_list[6], (NQ, MD), 0.25, 1.5, ((0, 512),))
    routes_keys = jax.random.split(jax.random.fold_in(key_list[7], 1), NQ // Q_DEV)
    routes_turns = jax.random.permutation(jax.random.fold_in(key_list[7], 3), NQ // Q_DEV)
    routes = jax.vmap(lambda own, number: routed_block(jax.random.fold_in(key_list[7], 2), own, number, Q_DEV, N_TX * N_TY, TOP, MOST, 2))(routes_keys, routes_turns).reshape((NQ, TOP))
    matched = with_ends(jax.random.randint(key_list[8], (NQ,), 0, NINST), jax.random.fold_in(key_list[8], 1), 0, NINST - 1).astype(jnp.int32)
    return dict(features=features, conv_weight=conv_weight, mask_weight=mask_weight, block_mask=block_mask, voxel_mask=voxel_mask, voxel_labels=voxel_labels, queries=queries, routes=routes, matched=matched)


def reference(features, conv_weight, mask_weight, block_mask, voxel_mask, voxel_labels, queries, routes, matched):
    expanded = jnp.repeat(jnp.repeat(jnp.repeat(block_mask, BX, axis=0), BY, axis=1), BZ, axis=2)
    occupied = expanded * voxel_mask
    masked = jnp.where(occupied[None] > 0, features, jnp.zeros_like(features))
    padded = jnp.pad(masked, ((0, 0), (1, 1), (1, 1), (1, 1)))
    conv_sum = jnp.zeros((CH, NX * NY * NZ), jnp.float32)
    for shift_x in range(3):
        for shift_y in range(3):
            for shift_z in range(3):
                offset_index = 9 * shift_x + 3 * shift_y + shift_z
                shifted = padded[:, shift_x:shift_x + NX, shift_y:shift_y + NY, shift_z:shift_z + NZ].reshape(CH, NX * NY * NZ)
                conv_sum = conv_sum + lax.dot_general(conv_weight[offset_index], shifted, (((0,), (0,)), ((), ())), preferred_element_type=jnp.float32)
    occupied_flat = occupied.reshape(-1).astype(jnp.float32)
    hidden = (jnp.maximum(conv_sum, 0.0) * occupied_flat[None, :]).astype(jnp.bfloat16)
    mask_features = lax.dot_general(mask_weight, hidden, (((0,), (0,)), ((), ())), preferred_element_type=jnp.float32).astype(jnp.bfloat16)
    tile_count = N_TX * N_TY
    tile_cells = CX * CY * NZ
    tile_features = mask_features.reshape(MD, N_TX, CX, N_TY, CY, NZ).transpose(1, 3, 0, 2, 4, 5).reshape(tile_count, MD, tile_cells)
    tile_labels = voxel_labels.reshape(N_TX, CX, N_TY, CY, NZ).transpose(0, 2, 1, 3, 4).reshape(tile_count, tile_cells)
    tile_occupied = occupied.reshape(N_TX, CX, N_TY, CY, NZ).transpose(0, 2, 1, 3, 4).reshape(tile_count, tile_cells).astype(jnp.float32)
    block_count = NQ // Q_DEV
    entry_count = Q_DEV * TOP
    block_routes = routes.reshape(block_count, entry_count)
    row_ids = jnp.arange(block_count, dtype=jnp.int32)[:, None] * Q_DEV + jnp.arange(entry_count, dtype=jnp.int32)[None, :] // TOP
    matched_entries = matched[row_ids]
    pair_weight = 1.0 / tile_cells
    slot_range = jnp.arange(MOST, dtype=jnp.int32)

    def tile_step(grads, inputs):
        tile_index, features_here, labels_here, occupied_here = inputs
        tile_hits = (block_routes == tile_index).astype(jnp.int32)
        slot_number = jnp.cumsum(tile_hits, axis=1, dtype=jnp.int32) - tile_hits
        chosen = tile_hits[:, :, None] * (slot_number[:, :, None] == slot_range[None, None, :]).astype(jnp.int32)
        live_slots = jnp.sum(chosen, axis=1, dtype=jnp.int32).reshape(-1)
        slot_query = jnp.sum(chosen * row_ids[:, :, None], axis=1, dtype=jnp.int32).reshape(-1)
        slot_instance = jnp.sum(chosen * matched_entries[:, :, None], axis=1, dtype=jnp.int32).reshape(-1) + live_slots - 1
        slot_queries = jnp.where(live_slots[:, None] > 0, queries[slot_query], jnp.zeros((1, MD), jnp.bfloat16))
        logits = jnp.dot(slot_queries, features_here, preferred_element_type=jnp.float32)
        target = (labels_here[None, :] == slot_instance[:, None]).astype(jnp.float32)
        slopes = ((jax.nn.sigmoid(logits) - target) * occupied_here[None, :] * pair_weight).astype(jnp.bfloat16)
        slot_grads = lax.dot_general(slopes, features_here, (((1,), (1,)), ((), ())), preferred_element_type=jnp.float32)
        slot_grads = jnp.where(live_slots[:, None] > 0, slot_grads, jnp.zeros_like(slot_grads))
        return grads.at[slot_query].add(slot_grads), None

    grads_start = jnp.zeros((NQ, MD), jnp.float32)
    query_grads, unused = lax.scan(tile_step, grads_start, (jnp.arange(tile_count, dtype=jnp.int32), tile_features, tile_labels, tile_occupied))
    return query_grads
```

```python
import jax
import jax.numpy as jnp
from jax import lax
from jax.experimental import pallas as pl
from jax.experimental.pallas import tpu as pltpu
from jax.sharding import PartitionSpec as P

F32 = jnp.float32
BF16 = jnp.bfloat16
CH = 32
MD = 128
TILES = 128
SLOTS = 256
NZ = 512
PB = 4
WEIGHT = 1.0 / 8192.0


def iota(shape, dim):
    return lax.broadcasted_iota(jnp.int32, shape, dim)


def mm(a, b):
    return jnp.dot(a, b, preferred_element_type=F32)


def onehot(cond):
    return jnp.where(cond, 1.0, 0.0).astype(BF16)


def earlier_rows():
    a, b = iota((128, 128), 0), iota((128, 128), 1)
    return onehot((a < b) & ((a >> 5) == (b >> 5)))


def send_kernel(pos_ref, routes_ref, queries_ref, out_ref, place_ref):
    tile, pb = pos_ref[0], pos_ref[1]
    own = routes_ref[tile]
    slot = iota((SLOTS, 128), 0)
    mine = (iota((SLOTS, 128), 1) >> 5) == pb
    named = jnp.zeros((SLOTS, 128), F32)
    for k in range(4):
        named = jnp.where((slot >> 1) == own[k : k + 1, :], 1.0, named)
    rank = mm(named.astype(BF16), earlier_rows())
    place = jnp.where(mine & (rank == (slot & 1).astype(F32)), named, 0.0).astype(BF16)
    place_ref[...] = place
    queries = queries_ref[...]
    stacked = jnp.concatenate([queries, queries, queries, queries], axis=0)
    out_ref[...] = mm(place, stacked).astype(BF16)


def mask_kernel(feat_ref, block_ref, vmask_ref, label_ref, out_ref):
    spread = onehot((iota((16, 128), 1) >> 3) == iota((16, 128), 0))
    blocks = jnp.broadcast_to(block_ref[...], (16, 16)).astype(F32).astype(BF16)
    occ = mm(blocks, spread) * vmask_ref[...].astype(F32)
    code = jnp.where(occ > 0.0, label_ref[...].astype(F32), -2.0).astype(BF16)
    rows, cols = iota((512, 512), 0), iota((512, 512), 1)
    perm = onehot(cols == ((rows & 31) * 16 + (rows >> 5)))
    moved = mm(perm, feat_ref[...])
    widen = onehot((iota((512, 16), 0) >> 5) == iota((512, 16), 1))
    occ_rows = mm(widen, occ.astype(BF16))
    masked = jnp.where(occ_rows > 0.0, moved, 0.0).astype(BF16)
    for c in range(PB):
        out_ref[c, 0:512, :] = masked
        out_ref[c, 512:528, :] = code


def weight_kernel(pos_ref, routes_ref, matched_ref, w_ref, mw_ref, inst_ref, t_ref, bd_ref, tt_ref):
    tile, pb = pos_ref[0], pos_ref[1]
    hits = jnp.zeros((TILES, 128), F32)
    for k in range(4):
        hits = jnp.where(routes_ref[:, k, :] == tile, 1.0, hits)
    hits = jnp.where((iota((TILES, 128), 1) >> 5) == pb, hits, 0.0)
    slot = iota((SLOTS, 128), 0)
    twice = onehot((slot >> 1) == iota((SLOTS, 128), 1))
    hits2 = mm(twice, hits.astype(BF16))
    insts = mm(twice, matched_ref[...].astype(F32).astype(BF16))
    rank = mm(hits2.astype(BF16), earlier_rows())
    chosen = jnp.where(rank == (slot & 1).astype(F32), hits2, 0.0)
    inst = jnp.sum(chosen * (insts + 1.0), axis=1, keepdims=True) - 1.0
    inst_ref[...] = jnp.broadcast_to(inst, (SLOTS, 128))
    spread = onehot((iota((CH, 128), 1) & 31) == iota((CH, 128), 0))
    wide = mm(w_ref[...], spread)
    group = iota((CH, 128), 1) >> 5
    for a in range(3):
        for yi in range(8):
            for c in range(3):
                part = jnp.zeros((CH, 128), F32)
                for b in range(3):
                    yo = yi - b
                    if 0 <= yo < 4:
                        at = (9 * a + 3 * b + c) * CH
                        part = jnp.where(group == yo, wide[at : at + CH, :], part)
                tt_ref[(a * 8 + yi) * CH : (a * 8 + yi + 1) * CH, c * 128 : (c + 1) * 128] = part
    for a in range(3):
        for c in range(3):
            part = tt_ref[a * 256 : (a + 1) * 256, c * 128 : (c + 1) * 128]
            t_ref[c * 128 : (c + 1) * 128, a * 256 : (a + 1) * 256] = part.T.astype(BF16)
    mw = mw_ref[...].astype(F32)
    mwt = jnp.concatenate([mw, mw, mw, mw], axis=0).T
    lane = iota((128, 128), 1) >> 5
    for yo in range(4):
        bd_ref[yo * 128 : (yo + 1) * 128, :] = jnp.where(lane == yo, mwt, 0.0).astype(BF16)


def face_kernel(own_ref, lo_ref, hi_ref, first_ref, last_ref):
    for c in range(PB):
        for ref, y in ((first_ref, 0), (last_ref, 3)):
            ref[c, 0:32, :] = lo_ref[c, y * 32 : y * 32 + 32, :]
            for x in range(4):
                at = x * 128 + y * 32
                ref[c, 32 + x * 32 : 64 + x * 32, :] = own_ref[c, at : at + 32, :]
            ref[c, 160:192, :] = hi_ref[c, y * 32 : y * 32 + 32, :]


def loss_kernel(
    own_ref, xlo_ref, xhi_ref, ylo_ref, yhi_ref, q_ref, inst_ref, t_ref, bd_ref, out_ref, x_ref
):
    for c in range(PB):
        z = slice(c * 128, (c + 1) * 128)
        for xi in range(6):
            base = xi * 256
            x_ref[base : base + 32, z] = ylo_ref[c, xi * 32 : xi * 32 + 32, :]
            if xi == 0:
                body = xlo_ref[c]
            elif xi == 5:
                body = xhi_ref[c]
            else:
                body = own_ref[c, (xi - 1) * 128 : xi * 128, :]
            x_ref[base + 32 : base + 160, z] = body
            x_ref[base + 160 : base + 192, z] = yhi_ref[c, xi * 32 : xi * 32 + 32, :]
            x_ref[base + 192 : base + 256, z] = jnp.zeros((64, 128), BF16)
    out_ref[...] = jnp.zeros((SLOTS, MD), F32)
    lane = iota((128, NZ), 1)
    zcol = iota((1, NZ), 1)
    inst = inst_ref[...]
    inst = jnp.concatenate([inst, inst, inst, inst], axis=1)
    half_q = (q_ref[...].astype(F32) * 0.5).astype(BF16)
    code_all = jnp.concatenate([own_ref[c, 512:528, :] for c in range(PB)], axis=1).astype(F32)

    for xo in range(4):
        parts = mm(t_ref[...], x_ref[xo * 256 : xo * 256 + 768, :])
        conv = parts[128:256]
        conv = conv + jnp.where(lane == 0, 0.0, pltpu.roll(parts[0:128], 1, 1))
        conv = conv + jnp.where(lane == NZ - 1, 0.0, pltpu.roll(parts[256:384], NZ - 1, 1))
        codes = code_all[xo * 4 : xo * 4 + 4]
        hidden = []
        for yo in range(4):
            occ = codes[yo : yo + 1] > -1.5
            hidden.append(jnp.where(occ, jnp.maximum(conv[yo * 32 : yo * 32 + 32], 0.0), 0.0))
        hidden = jnp.concatenate(hidden, axis=0).astype(BF16)
        feats = mm(bd_ref[...], hidden).astype(BF16)
        for yo in range(4):
            mf = feats[yo * 128 : (yo + 1) * 128]
            code = codes[yo : yo + 1]
            half_w = jnp.where(code > -1.5, 0.5 * WEIGHT, 0.0)
            half_t = jnp.tanh(mm(half_q, mf))
            base = jnp.where(code == inst, half_w - WEIGHT, half_w)
            slopes = (half_w * half_t + base).astype(BF16)
            out_ref[...] += lax.dot_general(
                slopes, mf, (((1,), (1,)), ((), ())), preferred_element_type=F32
            )


def home_kernel(pos_ref, place_ref, home_ref, out_ref):
    place = place_ref[...]
    home = home_ref[...]
    high = home.astype(BF16)
    rest = home - high.astype(F32)
    mid = rest.astype(BF16)
    low = (rest - mid.astype(F32)).astype(BF16)
    dims = (((0,), (0,)), ((), ()))
    total = jnp.zeros((128, MD), F32)
    for part in (low, mid, high):
        total = total + lax.dot_general(place, part, dims, preferred_element_type=F32)
    out_ref[...] = total[0:32] + total[32:64] + total[64:96] + total[96:128]


VM = pl.BlockSpec(memory_space=pltpu.VMEM)
SM = pl.BlockSpec(memory_space=pltpu.SMEM)


def call(kernel, outs, specs, scratch=()):
    return pl.pallas_call(
        kernel,
        out_shape=[jax.ShapeDtypeStruct(s, d) for s, d in outs],
        in_specs=specs,
        out_specs=[VM] * len(outs),
        scratch_shapes=list(scratch),
    )


def shifted(low_face, high_face, axis):
    count = lax.axis_size(axis)
    up = [(i, i + 1) for i in range(count - 1)]
    down = [(i + 1, i) for i in range(count - 1)]
    return lax.ppermute(high_face, axis, up), lax.ppermute(low_face, axis, down)


def body(features, conv_weight, mask_weight, block_mask, voxel_mask, voxel_labels, queries, routes, matched):
    tile = lax.axis_index("tx") * lax.axis_size("ty") + lax.axis_index("ty")
    pos = jnp.stack([tile, lax.axis_index("pb")]).astype(jnp.int32)
    routes_by_tile = routes.reshape(TILES, 128, 4).transpose(0, 2, 1)

    outgoing, place = call(
        send_kernel, [((SLOTS, MD), BF16), ((SLOTS, 128), BF16)], [SM, VM, VM]
    )(pos, routes_by_tile, queries)
    (own,) = call(mask_kernel, [((PB, 528, 128), BF16)], [VM] * 4)(
        features.reshape(512, 128),
        block_mask.reshape(1, 16),
        voxel_mask.reshape(16, 128),
        voxel_labels.reshape(16, 128),
    )
    arrived = lax.all_to_all(
        outgoing.reshape(TILES, 2, MD), ("tx", "ty"), split_axis=0, concat_axis=0, tiled=True
    ).reshape(SLOTS, MD)
    own = lax.all_to_all(own, "pb", split_axis=0, concat_axis=0, tiled=True)
    xlo, xhi = shifted(own[:, 0:128, :], own[:, 384:512, :], "tx")
    first, last = call(face_kernel, [((PB, 192, 128), BF16)] * 2, [VM] * 3)(own, xlo, xhi)
    ylo, yhi = shifted(first, last, "ty")
    inst, toeplitz, diag = call(
        weight_kernel,
        [((SLOTS, 128), F32), ((384, 768), BF16), ((512, 128), BF16)],
        [SM, VM, VM, VM, VM],
        [pltpu.VMEM((768, 384), F32)],
    )(pos, routes_by_tile, matched.reshape(TILES, 128), conv_weight.reshape(27 * CH, CH), mask_weight)
    (slot_grads,) = call(
        loss_kernel, [((SLOTS, MD), F32)], [VM] * 9, [pltpu.VMEM((6 * 256, NZ), BF16)]
    )(own, xlo, xhi, ylo, yhi, arrived, inst, toeplitz, diag)
    home = lax.all_to_all(
        slot_grads.reshape(TILES, 2, MD), ("tx", "ty"), split_axis=0, concat_axis=0, tiled=True
    ).reshape(SLOTS, MD)
    (grads,) = call(home_kernel, [((32, MD), F32)], [SM, VM, VM])(pos, place, home)
    return grads


def solution(mesh):
    placed = (
        P(None, "tx", "ty", "pb"),
        P(),
        P(),
        P("tx", "ty", "pb"),
        P("tx", "ty", "pb"),
        P("tx", "ty", "pb"),
        P(("tx", "ty", "pb"), None),
        P(),
        P(),
    )
    return jax.shard_map(
        body, mesh=mesh, in_specs=placed, out_specs=P(("tx", "ty", "pb"), None), check_vma=False
    )
```
